32 devices in a mesh: grp: 2 (over x), slab: 16 (over z, y, core).
Axes of the slice: x: 2, y: 2, z: 4, core: 2. Of those that a mesh axis runs over, the one named last changes fastest.
Arguments:
- right_side: bfloat16 [16, 12288, 128], P('grp', 'slab'), parts along dimension 0, may hold values from -6 to 6
- coupling: bfloat16 [96, 5, 2, 256, 128], P(('grp', 'slab')), parts along dimension 0, may hold values from -0.625 to 0.625
- diag_inverse: bfloat16 [96, 2, 256, 256], P(('grp', 'slab')), parts along dimension 0, may hold values from -0.125 to 0.125
- basis: bfloat16 [32, 2, 64, 256], P(('grp', 'slab')), parts along dimension 0, may hold values from -0.25 to 0.25
- near_tiles: int32 [48, 5], P('slab'), may hold values from 0 to 5, all different within a row
- far_basis: int32 [48, 2], P('slab'), may hold values from 0 to 15
Outputs:
- solution: bfloat16 [16, 12288, 128], P('grp', 'slab'), parts along dimension 0
The draws below stay inside these ranges and needn't reach their ends.
There are 2 independent parts, one for each index of `grp`. The reference program is written for one: setup_inputs(seed, part) draws one part's arguments, and reference() takes and returns one part's arrays. A program takes and returns all parts, laid end to end along the dimension named above; an argument that names none is the same for every part. Nothing has to cross between parts.
Inputs may be any that keep to these rules, and one draw needn't show every extreme that they name: `near_tiles`: each row names 5 different tiles.
All inputs are finite; a program needn't handle non-finite values.
Results may differ from the reference program's by a relative error of at most 0.038.
Values may be sent and summed in bfloat16 or wider, within the bound.
A program may use at most 64 MiB of HBM per device.

```python
import jax
import jax.numpy as jnp
from jax import lax

BLK = 256
TILE = 128
NEAR = 5
RANK = 64
BAND = 32
COLS = 128
BLOCKS = 3
TICKS = 8
SLABS = 16
ROWS = 768
TOTAL = 12288
NBLK = 48
NBASIS = 16


def set_ends(result, own_key, low, top_value):
    spot = [jax.random.randint(jax.random.fold_in(own_key, axis), (), 0, length) for axis, length in enumerate(result.shape)]
    main_axis = result.shape.index(max(result.shape))
    beside = spot[:main_axis] + [(spot[main_axis] + 1) % result.shape[main_axis]] + spot[main_axis + 1:]
    return result.at[tuple(spot)].set(low).at[tuple(beside)].set(top_value)


def block_scale(own_key, shape, split, low, largest):
    def one(axis_at, parts):
        draws = jax.random.uniform(jax.random.fold_in(jax.random.fold_in(own_key, 6), axis_at), (parts,), jnp.float32, low / len(split), largest / len(split))
        return jnp.repeat(jnp.exp(draws), shape[axis_at] // parts).reshape((-1,) + (1,) * (len(shape) - axis_at - 1))

    level = one(*split[0])
    for cut in split[1:]:
        level = level * one(*cut)
    return level


def different_ones(stream_key, rows, count, top, lift):
    ranking = jax.random.permutation(jax.random.fold_in(stream_key, 1), count)
    boost = ranking
    for power in range(3):
        boost = boost * boost // count
    boost = boost * lift // count
    lots = jax.random.randint(jax.random.fold_in(stream_key, 2), (rows, count), 0, 4096) + boost
    holders = jax.random.permutation(jax.random.fold_in(stream_key, 3), rows)[jnp.arange(count) % rows]
    lots = jnp.where(jnp.arange(rows)[:, None] == holders[None, :], 1 << 14, lots)
    merit = lots * count + jnp.arange(count)
    return lax.top_k(merit.astype(jnp.int32), top)[1].astype(jnp.int32)


def bell_draw(rng, shape, scale, limit, pieces=(), kind=jnp.bfloat16):
    result = jax.random.normal(rng, shape, jnp.float32) * scale
    if len(pieces) > 0:
        result = block_scale(rng, shape, pieces, -0.22, 0.18) * result
    return jnp.clip(result, min=-limit, max=limit).astype(kind)


def setup_inputs(seed: int = 0, part: int = 0) -> dict:
    keys = jax.random.split(jax.random.key(seed), 7)
    part_splits = jax.random.split(jax.random.fold_in(keys[6], part), 7)
    right_side = bell_draw(part_splits[0], (TICKS, TOTAL, COLS), 1.0, 6.0, ((1, 16),))
    coupling = bell_draw(part_splits[1], (NBLK, NEAR, 2, BLK, TILE), (NEAR * TILE // 8) ** -0.5, 0.625, ((0, 16),))
    diag_inverse = bell_draw(part_splits[2], (NBLK, 2, BLK, BLK), (32 * (2 * BAND + 1)) ** -0.5, 0.125, ((0, 16),))
    basis = bell_draw(part_splits[3], (NBASIS, 2, RANK, BLK), (2 * BLK) ** -0.5, 0.25, ((0, 16),))
    near_tiles = different_ones(keys[4], NBLK, ROWS // TILE, NEAR, 0)
    far_basis = set_ends(jax.random.randint(keys[5], (NBLK, 2), 0, NBASIS), jax.random.fold_in(keys[5], 1), 0, NBASIS - 1).astype(jnp.int32)
    return {"right_side": right_side, "coupling": coupling, "diag_inverse": diag_inverse, "basis": basis, "near_tiles": near_tiles, "far_basis": far_basis}


def rotate(values):
    half_cols = values.shape[-1] // 2
    return jnp.concatenate([-values[..., half_cols:], values[..., :half_cols]], axis=-1)

def paired(values, position):
    return jnp.stack([values, rotate(values)], axis=position)

def reference(right_side, coupling, diag_inverse, basis, near_tiles, far_basis):
    highest = lax.Precision.HIGHEST
    slab_rows = BLOCKS * BLK
    offsets = jnp.arange(BLK)[:, None] - jnp.arange(BLK)[None, :]
    inside = jnp.abs(offsets) <= BAND
    banded = jnp.where(inside, diag_inverse, jnp.zeros_like(diag_inverse))
    picked = jnp.take(basis, far_basis, axis=0)
    per_slab = (jnp.moveaxis(right_side.reshape(TICKS, SLABS, slab_rows, COLS), 1, 0), coupling.reshape(SLABS, BLOCKS, NEAR, 2, BLK, TILE), banded.reshape(SLABS, BLOCKS, 2, BLK, BLK), picked.reshape(SLABS, BLOCKS, 2, 2, RANK, BLK), near_tiles.reshape(SLABS, BLOCKS, NEAR), jnp.arange(SLABS, dtype=jnp.int32))

    def advance(carried, slab_data):
        panel, accum = carried
        slab_side, slab_coupling, slab_band, slab_basis, slab_tiles, slab_index = slab_data
        far_scale = 1.0 / jnp.sqrt((BLOCKS * jnp.maximum(slab_index, 1)).astype(jnp.float32))
        previous = panel.reshape(TICKS, slab_rows // TILE, TILE, COLS)
        chosen = previous[:, slab_tiles]
        near_term = jnp.einsum('bnprt,gbnptc->gbrc', slab_coupling.astype(jnp.float32), paired(chosen, 3).astype(jnp.float32), precision=highest)
        far_field = accum.astype(jnp.bfloat16)
        far_term = jnp.einsum('bpkr,gpkc->gbrc', slab_basis[:, 1].astype(jnp.float32), paired(far_field, 1).astype(jnp.float32), precision=highest) * far_scale
        modified = (slab_side.reshape(TICKS, BLOCKS, BLK, COLS).astype(jnp.float32) - near_term - far_term).astype(jnp.bfloat16)
        solved = jnp.einsum('bprs,gbpsc->gbrc', slab_band.astype(jnp.float32), paired(modified, 2).astype(jnp.float32), precision=highest).astype(jnp.bfloat16)
        coefficients = jnp.einsum('bpkr,gbprc->gkc', slab_basis[:, 0].astype(jnp.float32), paired(solved, 2).astype(jnp.float32), precision=highest)
        solved_rows = solved.reshape(TICKS, slab_rows, COLS)
        return ((solved_rows, accum + coefficients), solved_rows)
    start_state = (jnp.zeros((TICKS, slab_rows, COLS), jnp.bfloat16), jnp.zeros((TICKS, RANK, COLS), jnp.float32))
    final_state, solved_all = lax.scan(advance, start_state, per_slab)
    return jnp.moveaxis(solved_all, 0, 1).reshape(TICKS, SLABS * slab_rows, COLS)
```

```python
import functools

import jax
import jax.numpy as jnp
from jax import lax
from jax.experimental import pallas as pl
from jax.experimental.pallas import tpu as pltpu
from jax.sharding import PartitionSpec as P

BAND = 32
MESH = pl.DeviceIdType.MESH
F32 = jnp.float32
BF16 = jnp.bfloat16


def turned(values):
    half = values.shape[-1] // 2
    rolled = pltpu.roll(values, half, 1)
    lane = lax.broadcasted_iota(jnp.int32, values.shape, 1)
    return jnp.where(lane < half, -rolled, rolled)


def complex_sum(stacked):
    rows = stacked.shape[0] // 2
    return stacked[:rows] + turned(stacked[rows:])


def mul(a, b):
    return jnp.dot(a, b, preferred_element_type=F32)


def kernel(
    n, rs, cp, di, ba, nt, fb, scale, out,
    gath, w, ds, bd, nn, y, vbuf, sbuf, gs, gr, cs, cr,
):
    blocks, near, _, blk, tile = cp.shape
    ticks, rows, _ = rs.shape
    rank = ba.shape[2]
    tiles = rows // tile
    two = 2 * blk
    me = lax.axis_index("slab")
    depth = n // 4
    z, q = me // 4, me % 4
    across = z * 4 + (q + 2) % 4
    beside = me + 1 - 2 * (q % 2)

    barrier = pltpu.get_barrier_semaphore()

    def greet(there, who):
        @pl.when(there)
        def _():
            pl.semaphore_signal(barrier, inc=1, device_id={"slab": who}, device_id_type=MESH)

    sides = (
        (me > 0, me - 1),
        (me < n - 1, me + 1),
        (z > 0, me - 4),
        (z < depth - 1, me + 4),
        (me >= 0, across),
    )
    for there, who in sides:
        greet(there, who)
    pl.semaphore_wait(barrier, sum(there.astype(jnp.int32) for there, _ in sides))

    def basis_copy(way, slot, who, own=False):
        return pltpu.make_async_remote_copy(
            src_ref=ba.at[0] if own else gath.at[slot],
            dst_ref=gath.at[slot],
            send_sem=gs.at[way, slot],
            recv_sem=gr.at[slot],
            device_id={"slab": who},
            device_id_type=MESH,
        )

    def arrived(slot):
        basis_copy(0, slot, beside).wait_recv()

    def own_out(finish):
        def one(there, way, who):
            @pl.when(there)
            def _():
                copy = basis_copy(way, me, who, own=True)
                copy.wait_send() if finish else copy.start()

        one(z < depth - 1, 0, me + 4)
        one(z > 0, 1, me - 4)
        one(me >= 0, 2, across)
        one(me >= 0, 3, beside)

    def line(k, finish):
        def one(there, way, who, slot):
            @pl.when(there)
            def _():
                copy = basis_copy(way, slot, who)
                copy.wait_send() if finish else copy.start()

        low, high = me - 4 * k, me + 4 * k

        @pl.when(z >= k)
        def _():
            if not finish:
                arrived(low)
            one(z < depth - 1, 0, me + 4, low)
            one(me >= 0, 2, across, low)
            one(me >= 0, 3, beside, low)

        @pl.when(z + k < depth)
        def _():
            if not finish:
                arrived(high)
            one(z > 0, 1, me - 4, high)
            one(me >= 0, 2, across, high)
            one(me >= 0, 3, beside, high)

    def other_line(k, finish):
        slot = k * 4 + (q + 2) % 4
        copy = basis_copy(3, slot, beside)
        if finish:
            copy.wait_send()
        else:
            arrived(slot)
            copy.start()

    def others_in(k):
        arrived(k * 4 + beside % 4)
        arrived(k * 4 + (beside + 2) % 4)

    own_out(False)
    gath[me] = ba[0]

    offset = lax.broadcasted_iota(jnp.int32, (blk, blk), 0) - lax.broadcasted_iota(
        jnp.int32, (blk, blk), 1
    )
    inside = jnp.abs(offset) <= BAND
    for b in range(blocks):
        for p in range(2):
            part = jnp.where(inside, di[b, p].astype(F32), 0.0)
            ds[b, p * blk : (p + 1) * blk, 0:blk] = part.astype(BF16)
            other = part if p == 0 else -part
            ds[b, (1 - p) * blk : (2 - p) * blk, blk:two] = other.astype(BF16)

    def near_block(b):
        for j in range(tiles):
            place, held = jnp.int32(0), jnp.int32(0)
            for m in range(near):
                hit = (nt[b, m] == j).astype(jnp.int32)
                place = jnp.maximum(place, m * hit)
                held = jnp.maximum(held, hit)
            keep = held.astype(F32)
            for p in range(2):
                piece = cp[b, place, p].astype(F32) * keep
                nn[p * blk : (p + 1) * blk, j * tile : (j + 1) * tile] = piece.astype(BF16)
        w[b * two : (b + 1) * two, 0:rows] = mul(ds[b], nn[...]).astype(BF16)

    near_block(0)
    for k in range(1, blocks):
        line(k, False)
        near_block(k)

    def line_loop(k, carry):
        line(k, False)
        return carry

    lax.fori_loop(blocks, depth, line_loop, 0)

    def other_loop(k, carry):
        other_line(k, False)
        return carry

    lax.fori_loop(0, depth, other_loop, 0)

    def side_tick(t, carry):
        for b in range(blocks):
            piece = rs[t, b * blk : (b + 1) * blk, :]
            y[t, b * blk : (b + 1) * blk, :] = complex_sum(mul(ds[b, :, 0:blk], piece))
        return carry

    lax.fori_loop(0, ticks, side_tick, 0)

    def others_loop(k, carry):
        others_in(k)
        return carry

    lax.fori_loop(0, depth, others_loop, 0)

    total = jnp.zeros((2 * rank, rows + rank), F32)
    for b in range(blocks):
        far = jnp.concatenate([gath[fb[b, 1], 0], gath[fb[b, 1], 1]], axis=1)
        spread = lax.dot_general(
            ds[b], far, (((1,), (1,)), ((), ())), preferred_element_type=F32
        )
        w[b * two : (b + 1) * two, rows : rows + rank] = (spread * scale[0]).astype(BF16)
        real, imag = gath[fb[b, 0], 0], gath[fb[b, 0], 1]
        both = jnp.concatenate(
            [
                jnp.concatenate([real, -imag], axis=1),
                jnp.concatenate([imag, real], axis=1),
            ],
            axis=0,
        )
        total = total + mul(both, w[b * two : (b + 1) * two, :])
        bd[b] = mul(both, ds[b, :, 0:blk]).astype(BF16)
    w[blocks * two : blocks * two + 2 * rank, :] = total.astype(BF16)

    def gain_tick(t, carry):
        gain = jnp.zeros((2 * rank, rs.shape[2]), F32)
        for b in range(blocks):
            gain = gain + mul(bd[b], rs[t, b * blk : (b + 1) * blk, :])
        y[t, rows : rows + rank, :] = complex_sum(gain)
        return carry

    lax.fori_loop(0, ticks, gain_tick, 0)

    @pl.when(me == 0)
    def _():
        vbuf[...] = jnp.zeros_like(vbuf)

    def chain_copy(t, c):
        first = c * blk
        count = blk if c < blocks else rank
        return pltpu.make_async_remote_copy(
            src_ref=sbuf.at[t, pl.ds(first, count)],
            dst_ref=vbuf.at[t, pl.ds(first, count)],
            send_sem=cs.at[t, c],
            recv_sem=cr.at[t, c],
            device_id={"slab": me + 1},
            device_id_type=MESH,
        )

    def tick(t, carry):
        @pl.when(me > 0)
        def _():
            for c in range(blocks + 1):
                chain_copy(t, c).wait_recv()

        state = vbuf[t]
        for b in range(blocks):
            part = slice(b * blk, (b + 1) * blk)
            solved = y[t, part, :] - complex_sum(mul(w[b * two : (b + 1) * two, :], state))
            solved = solved.astype(BF16)
            out[t, part, :] = solved
            sbuf[t, part, :] = solved

            @pl.when(me < n - 1)
            def _():
                chain_copy(t, b).start()

        part = slice(rows, rows + rank)
        gained = y[t, part, :] - complex_sum(mul(w[blocks * two :, :], state))
        sbuf[t, part, :] = (vbuf[t, part, :].astype(F32) + gained).astype(BF16)

        @pl.when(me < n - 1)
        def _():
            chain_copy(t, blocks).start()

        return carry

    lax.fori_loop(0, ticks, tick, 0)

    def chain_end(t, carry):
        for c in range(blocks + 1):
            chain_copy(t, c).wait_send()
        return carry

    @pl.when(me < n - 1)
    def _():
        lax.fori_loop(0, ticks, chain_end, 0)

    own_out(True)

    def line_end(k, carry):
        line(k, True)
        return carry

    lax.fori_loop(1, depth, line_end, 0)

    def other_end(k, carry):
        other_line(k, True)
        return carry

    lax.fori_loop(0, depth, other_end, 0)


def body(right_side, coupling, diag_inverse, basis, near_tiles, far_basis):
    blocks, _, _, blk, _ = coupling.shape
    ticks, rows, columns = right_side.shape
    rank = basis.shape[2]
    n = lax.axis_size("slab")
    earlier = blocks * jnp.maximum(lax.axis_index("slab"), 1)
    scale = (1.0 / jnp.sqrt(earlier.astype(F32))).reshape(1)
    vmem = pl.BlockSpec(memory_space=pltpu.VMEM)
    smem = pl.BlockSpec(memory_space=pltpu.SMEM)
    return pl.pallas_call(
        functools.partial(kernel, n),
        out_shape=jax.ShapeDtypeStruct(right_side.shape, right_side.dtype),
        in_specs=[vmem] * 4 + [smem] * 3,
        out_specs=vmem,
        scratch_shapes=[
            pltpu.VMEM((n,) + basis.shape[1:], BF16),
            pltpu.VMEM((2 * (rows + rank), rows + rank), BF16),
            pltpu.VMEM((blocks, 2 * blk, 2 * blk), BF16),
            pltpu.VMEM((blocks, 2 * rank, blk), BF16),
            pltpu.VMEM((2 * blk, rows), BF16),
            pltpu.VMEM((ticks, rows + rank, columns), F32),
            pltpu.VMEM((ticks, rows + rank, columns), BF16),
            pltpu.VMEM((ticks, rows + rank, columns), BF16),
            pltpu.SemaphoreType.DMA((4, n)),
            pltpu.SemaphoreType.DMA((n,)),
            pltpu.SemaphoreType.DMA((ticks, blocks + 1)),
            pltpu.SemaphoreType.DMA((ticks, blocks + 1)),
        ],
        compiler_params=pltpu.CompilerParams(
            collective_id=0, has_side_effects=True, vmem_limit_bytes=48 * 1024 * 1024
        ),
    )(right_side, coupling, diag_inverse, basis, near_tiles, far_basis, scale)


def solution(mesh):
    placed = (
        P("grp", "slab", None),
        P(("grp", "slab"), None, None, None, None),
        P(("grp", "slab"), None, None, None),
        P(("grp", "slab"), None, None, None),
        P("slab", None),
        P("slab", None),
    )
    return jax.shard_map(
        body, mesh=mesh, in_specs=placed, out_specs=P("grp", "slab", None), check_vma=False
    )
```

```python
import functools

import jax
import jax.numpy as jnp
from jax import lax
from jax.experimental import pallas as pl
from jax.experimental.pallas import tpu as pltpu
from jax.sharding import PartitionSpec as P

BAND = 32
MESH = pl.DeviceIdType.MESH
F32 = jnp.float32
BF16 = jnp.bfloat16


def turned(values):
    half = values.shape[-1] // 2
    rolled = pltpu.roll(values, half, 1)
    lane = lax.broadcasted_iota(jnp.int32, values.shape, 1)
    return jnp.where(lane < half, -rolled, rolled)


def complex_sum(stacked):
    rows = stacked.shape[0] // 2
    return stacked[:rows] + turned(stacked[rows:])


def mul(a, b):
    return jnp.dot(a, b, preferred_element_type=F32)


def kernel(
    n, rs_in, cp_in, di_in, ba_in, nt, fb, scale, out,
    rs, cp, di, ba, gath, w, ds, bd, nn, y, acc, vbuf, sbuf, gs, gr, cs, cr, inn, outs,
):
    loads = [
        pltpu.make_async_copy(src, dst, inn.at[k])
        for k, (src, dst) in enumerate(((ba_in, ba), (di_in, di), (cp_in, cp), (rs_in, rs)))
    ]
    for load in loads:
        load.start()
    blocks, near, _, blk, tile = cp.shape
    ticks, rows, _ = rs.shape
    rank = ba.shape[2]
    tiles = rows // tile
    two = 2 * blk
    me = lax.axis_index("slab")
    depth = n // 4
    z, q = me // 4, me % 4
    across = z * 4 + (q + 2) % 4
    beside = me + 1 - 2 * (q % 2)

    def first(b):
        return b * blk + (rank if b else 0)

    def span(b):
        return slice(first(b), first(b) + blk)

    def sent(b):
        return blk if b else blk + rank

    def col(b):
        return b * two + (2 * rank if b else 0)

    extra = slice(blk, blk + rank)
    extra_col = slice(two, two + 2 * rank)
    barrier = pltpu.get_barrier_semaphore()

    def greet(there, who):
        @pl.when(there)
        def _():
            pl.semaphore_signal(barrier, inc=1, device_id={"slab": who}, device_id_type=MESH)

    sides = (
        (me > 0, me - 1),
        (me < n - 1, me + 1),
        (z > 0, me - 4),
        (z < depth - 1, me + 4),
        (me >= 0, across),
    )
    for there, who in sides:
        greet(there, who)
    pl.semaphore_wait(barrier, sum(there.astype(jnp.int32) for there, _ in sides))

    def basis_copy(way, slot, who, own=False):
        return pltpu.make_async_remote_copy(
            src_ref=ba.at[0] if own else gath.at[slot],
            dst_ref=gath.at[slot],
            send_sem=gs.at[way, slot],
            recv_sem=gr.at[slot],
            device_id={"slab": who},
            device_id_type=MESH,
        )

    def arrived(slot):
        basis_copy(0, slot, beside).wait_recv()

    def own_out(finish):
        def one(there, way, who):
            @pl.when(there)
            def _():
                copy = basis_copy(way, me, who, own=True)
                copy.wait_send() if finish else copy.start()

        one(z < depth - 1, 0, me + 4)
        one(z > 0, 1, me - 4)
        one(me >= 0, 2, across)
        one(me >= 0, 3, beside)

    def line(k, finish):
        def one(there, way, who, slot):
            @pl.when(there)
            def _():
                copy = basis_copy(way, slot, who)
                copy.wait_send() if finish else copy.start()

        low, high = me - 4 * k, me + 4 * k

        @pl.when(z >= k)
        def _():
            if not finish:
                arrived(low)
            one(z < depth - 1, 0, me + 4, low)
            one(me >= 0, 2, across, low)
            one(me >= 0, 3, beside, low)

        @pl.when(z + k < depth)
        def _():
            if not finish:
                arrived(high)
            one(z > 0, 1, me - 4, high)
            one(me >= 0, 2, across, high)
            one(me >= 0, 3, beside, high)

    def other_line(k, finish):
        slot = k * 4 + (q + 2) % 4
        copy = basis_copy(3, slot, beside)
        if finish:
            copy.wait_send()
        else:
            arrived(slot)
            copy.start()

    def others_in(k):
        arrived(k * 4 + beside % 4)
        arrived(k * 4 + (beside + 2) % 4)

    loads[0].wait()
    own_out(False)
    gath[me] = ba[0]
    loads[1].wait()

    offset = lax.broadcasted_iota(jnp.int32, (blk, blk), 0) - lax.broadcasted_iota(
        jnp.int32, (blk, blk), 1
    )
    inside = jnp.abs(offset) <= BAND
    for b in range(blocks):
        for p in range(2):
            part = jnp.where(inside, di[b, p].astype(F32), 0.0)
            ds[b, p * blk : (p + 1) * blk, 0:blk] = part.astype(BF16)
            other = part if p == 0 else -part
            ds[b, (1 - p) * blk : (2 - p) * blk, blk:two] = other.astype(BF16)

    def near_block(b):
        for j in range(tiles):
            place, held = jnp.int32(0), jnp.int32(0)
            for m in range(near):
                hit = (nt[b, m] == j).astype(jnp.int32)
                place = jnp.maximum(place, m * hit)
                held = jnp.maximum(held, hit)
            keep = held.astype(F32)
            for p in range(2):
                piece = cp[b, place, p].astype(F32) * keep
                nn[p * blk : (p + 1) * blk, j * tile : (j + 1) * tile] = piece.astype(BF16)
        whole = mul(ds[b], nn[...]).astype(BF16)
        for i in range(blocks):
            at = slice(i * blk, (i + 1) * blk)
            w[span(b), col(i) : col(i) + blk] = whole[0:blk, at]
            w[span(b), col(i) + blk : col(i) + two] = whole[blk:two, at]

    loads[2].wait()
    near_block(0)
    for k in range(1, blocks):
        line(k, False)
        near_block(k)

    def line_loop(k, carry):
        line(k, False)
        return carry

    lax.fori_loop(blocks, depth, line_loop, 0)

    def other_loop(k, carry):
        other_line(k, False)
        return carry

    lax.fori_loop(0, depth, other_loop, 0)

    def side_tick(t, carry):
        for b in range(blocks):
            piece = rs[t, b * blk : (b + 1) * blk, :]
            y[t, span(b), :] = complex_sum(mul(ds[b, :, 0:blk], piece))
        return carry

    loads[3].wait()
    lax.fori_loop(0, ticks, side_tick, 0)

    def others_loop(k, carry):
        others_in(k)
        return carry

    lax.fori_loop(0, depth, others_loop, 0)

    for b in range(blocks):
        real, imag = gath[fb[b, 0], 0], gath[fb[b, 0], 1]
        bd[b, :, 0:two] = jnp.concatenate([real, -imag], axis=1)
        low = jnp.concatenate([imag, real], axis=1)
        both = jnp.concatenate([bd[b, :, 0:two], low], axis=0)
        pair = mul(both, ds[b, :, 0:blk]).astype(BF16)
        bd[b, :, two : two + blk] = pair[0:rank]
        bd[b, :, two + blk : 2 * two] = pair[rank : 2 * rank]

    def gain(t):
        real = jnp.zeros((rank, rs.shape[2]), F32)
        imag = jnp.zeros((rank, rs.shape[2]), F32)
        for b in range(blocks):
            piece = rs[t, b * blk : (b + 1) * blk, :]
            real = real + mul(bd[b, :, two : two + blk], piece)
            imag = imag + mul(bd[b, :, two + blk : 2 * two], piece)
        y[t, extra, :] = real + turned(imag)

    def chain_copy(t, c):
        at = pl.ds(first(c), sent(c))
        return pltpu.make_async_remote_copy(
            src_ref=sbuf.at[t, at],
            dst_ref=vbuf.at[t, at],
            send_sem=cs.at[t, c],
            recv_sem=cr.at[t, c],
            device_id={"slab": me + 1},
            device_id_type=MESH,
        )

    def out_copy(t, c):
        return pltpu.make_async_copy(
            sbuf.at[t, pl.ds(first(c), blk)], out.at[t, pl.ds(c * blk, blk)], outs.at[t, c]
        )

    def give(t, c, values):
        sbuf[t, first(c) : first(c) + sent(c), :] = values.astype(BF16)

        @pl.when(me < n - 1)
        def _():
            chain_copy(t, c).start()

        out_copy(t, c).start()

    @pl.when(me == 0)
    def _():
        def tick(t, carry):
            gain(t)
            for b in range(blocks):
                give(t, b, y[t, first(b) : first(b) + sent(b), :])
            return carry

        lax.fori_loop(0, ticks, tick, 0)

    @pl.when(me > 0)
    def _():
        for b in range(blocks):
            real, imag = gath[fb[b, 1], 0], gath[fb[b, 1], 1]
            far = jnp.concatenate(
                [
                    jnp.concatenate([real, imag], axis=1),
                    jnp.concatenate([imag, -real], axis=1),
                ],
                axis=0,
            )
            spread = lax.dot_general(
                ds[b, 0:blk, :], far, (((1,), (1,)), ((), ())), preferred_element_type=F32
            )
            w[span(b), extra_col] = (spread * scale[0]).astype(BF16)

        for i in range(blocks):
            total = jnp.zeros((2 * rank, blk), F32)
            for b in range(blocks):
                up = bd[b, :, 0:two]
                down = jnp.concatenate([-up[:, blk:two], up[:, 0:blk]], axis=1)
                stack = jnp.concatenate(
                    [w[span(b), col(i) : col(i) + blk], w[span(b), col(i) + blk : col(i) + two]],
                    axis=0,
                )
                total = total + mul(jnp.concatenate([up, down], axis=0), stack)
            w[extra, col(i) : col(i) + blk] = total[0:rank].astype(BF16)
            w[extra, col(i) + blk : col(i) + two] = total[rank : 2 * rank].astype(BF16)
        total = jnp.zeros((rank, 2 * rank), F32)
        for b in range(blocks):
            spread = w[span(b), extra_col]
            swapped = turned(spread.astype(F32)).astype(BF16)
            total = total + mul(bd[b, :, 0:blk], spread) - mul(bd[b, :, blk:two], swapped)
        w[extra, extra_col] = total.astype(BF16)

        def gain_tick(t, carry):
            gain(t)
            return carry

        lax.fori_loop(0, ticks, gain_tick, 0)

        def tick(t, carry):
            for c in range(blocks):
                chain_copy(t, c).wait_recv()
                piece = vbuf[t, span(c), :]
                parts = [piece, turned(piece.astype(F32)).astype(BF16)]
                if c == 0:
                    field = vbuf[t, extra, :].astype(F32)
                    parts += [field.astype(BF16), turned(field).astype(BF16)]
                state = jnp.concatenate(parts, axis=0)
                cols = slice(col(c), col(c) + state.shape[0])
                if c < blocks - 1:
                    old = y[t] if c == 0 else acc[...]
                    acc[...] = old - mul(w[:, cols], state)
                    if c == 0:
                        acc[extra, :] = acc[extra, :] + field
                else:
                    for b in range(blocks):
                        at = slice(first(b), first(b) + sent(b))
                        give(t, b, acc[at, :] - mul(w[at, cols], state))
            return carry

        lax.fori_loop(0, ticks, tick, 0)

    def chain_end(t, carry):
        for c in range(blocks):
            out_copy(t, c).wait()

            @pl.when(me < n - 1)
            def _():
                chain_copy(t, c).wait_send()

        return carry

    lax.fori_loop(0, ticks, chain_end, 0)

    own_out(True)

    def line_end(k, carry):
        line(k, True)
        return carry

    lax.fori_loop(1, depth, line_end, 0)

    def other_end(k, carry):
        other_line(k, True)
        return carry

    lax.fori_loop(0, depth, other_end, 0)


def body(right_side, coupling, diag_inverse, basis, near_tiles, far_basis):
    blocks, _, _, blk, _ = coupling.shape
    ticks, rows, columns = right_side.shape
    rank = basis.shape[2]
    n = lax.axis_size("slab")
    earlier = blocks * jnp.maximum(lax.axis_index("slab"), 1)
    scale = (1.0 / jnp.sqrt(earlier.astype(F32))).reshape(1)
    anywhere = pl.BlockSpec(memory_space=pl.ANY)
    smem = pl.BlockSpec(memory_space=pltpu.SMEM)
    return pl.pallas_call(
        functools.partial(kernel, n),
        out_shape=jax.ShapeDtypeStruct(right_side.shape, right_side.dtype),
        in_specs=[anywhere] * 4 + [smem] * 3,
        out_specs=anywhere,
        scratch_shapes=[
            pltpu.VMEM(right_side.shape, BF16),
            pltpu.VMEM(coupling.shape, BF16),
            pltpu.VMEM(diag_inverse.shape, BF16),
            pltpu.VMEM(basis.shape, BF16),
            pltpu.VMEM((n,) + basis.shape[1:], BF16),
            pltpu.VMEM((rows + rank, 2 * (rows + rank)), BF16),
            pltpu.VMEM((blocks, 2 * blk, 2 * blk), BF16),
            pltpu.VMEM((blocks, rank, 4 * blk), BF16),
            pltpu.VMEM((2 * blk, rows), BF16),
            pltpu.VMEM((ticks, rows + rank, columns), F32),
            pltpu.VMEM((rows + rank, columns), F32),
            pltpu.VMEM((ticks, rows + rank, columns), BF16),
            pltpu.VMEM((ticks, rows + rank, columns), BF16),
            pltpu.SemaphoreType.DMA((4, n)),
            pltpu.SemaphoreType.DMA((n,)),
            pltpu.SemaphoreType.DMA((ticks, blocks)),
            pltpu.SemaphoreType.DMA((ticks, blocks)),
            pltpu.SemaphoreType.DMA((4,)),
            pltpu.SemaphoreType.DMA((ticks, blocks)),
        ],
        compiler_params=pltpu.CompilerParams(
            collective_id=0, has_side_effects=True, vmem_limit_bytes=60 * 1024 * 1024
        ),
    )(right_side, coupling, diag_inverse, basis, near_tiles, far_basis, scale)


def solution(mesh):
    placed = (
        P("grp", "slab", None),
        P(("grp", "slab"), None, None, None, None),
        P(("grp", "slab"), None, None, None),
        P(("grp", "slab"), None, None, None),
        P("slab", None),
        P("slab", None),
    )
    return jax.shard_map(
        body, mesh=mesh, in_specs=placed, out_specs=P("grp", "slab", None), check_vma=False
    )
```

```python
import functools

import jax
import jax.numpy as jnp
from jax import lax
from jax.experimental import pallas as pl
from jax.experimental.pallas import tpu as pltpu
from jax.sharding import PartitionSpec as P

BAND = 32
MESH = pl.DeviceIdType.MESH
F32 = jnp.float32
BF16 = jnp.bfloat16


def turned(values):
    half = values.shape[-1] // 2
    rolled = pltpu.roll(values, half, 1)
    lane = lax.broadcasted_iota(jnp.int32, values.shape, 1)
    return jnp.where(lane < half, -rolled, rolled)


def complex_sum(stacked):
    rows = stacked.shape[0] // 2
    return stacked[:rows] + turned(stacked[rows:])


def mul(a, b):
    return jnp.dot(a, b, preferred_element_type=F32)


def kernel(
    n, rs_in, cp_in, di_in, ba_in, nt, fb, scale, out,
    rs, cp, di, ba, gath, w, ds, bd, nn, y, acc, vbuf, sbuf, gs, gr, cs, cr, inn, outs,
):
    loads = [
        pltpu.make_async_copy(src, dst, inn.at[k])
        for k, (src, dst) in enumerate(((ba_in, ba), (di_in, di), (cp_in, cp)))
    ] + [
        pltpu.make_async_copy(
            rs_in.at[t], rs.at[:, pl.ds(t * rs_in.shape[2], rs_in.shape[2])], inn.at[3 + t]
        )
        for t in range(rs_in.shape[0])
    ]
    for load in loads:
        load.start()
    blocks, near, _, blk, tile = cp.shape
    ticks, rows, columns = rs_in.shape
    batch = 4 if ticks % 4 == 0 else 1
    rank = ba.shape[2]
    tiles = rows // tile
    two = 2 * blk
    me = lax.axis_index("slab")
    depth = n // 4
    z, q = me // 4, me % 4
    across = z * 4 + (q + 2) % 4
    beside = me + 1 - 2 * (q % 2)

    def first(b):
        return b * blk + (rank if b else 0)

    def span(b):
        return slice(first(b), first(b) + blk)

    def sent(b):
        return blk if b else blk + rank

    def col(b):
        return b * two + (2 * rank if b else 0)

    extra = slice(blk, blk + rank)
    extra_col = slice(two, two + 2 * rank)
    barrier = pltpu.get_barrier_semaphore()

    def greet(there, who):
        @pl.when(there)
        def _():
            pl.semaphore_signal(barrier, inc=1, device_id={"slab": who}, device_id_type=MESH)

    sides = (
        (me > 0, me - 1),
        (me < n - 1, me + 1),
        (z > 0, me - 4),
        (z < depth - 1, me + 4),
        (me >= 0, across),
    )
    for there, who in sides:
        greet(there, who)
    pl.semaphore_wait(barrier, sum(there.astype(jnp.int32) for there, _ in sides))

    def basis_copy(way, slot, who, own=False):
        return pltpu.make_async_remote_copy(
            src_ref=ba.at[0] if own else gath.at[slot],
            dst_ref=gath.at[slot],
            send_sem=gs.at[way, slot],
            recv_sem=gr.at[slot],
            device_id={"slab": who},
            device_id_type=MESH,
        )

    def arrived(slot):
        basis_copy(0, slot, beside).wait_recv()

    def own_out(finish):
        def one(there, way, who):
            @pl.when(there)
            def _():
                copy = basis_copy(way, me, who, own=True)
                copy.wait_send() if finish else copy.start()

        one(z < depth - 1, 0, me + 4)
        one(z > 0, 1, me - 4)
        one(me >= 0, 2, across)
        one(me >= 0, 3, beside)

    def line(k, finish):
        def one(there, way, who, slot):
            @pl.when(there)
            def _():
                copy = basis_copy(way, slot, who)
                copy.wait_send() if finish else copy.start()

        low, high = me - 4 * k, me + 4 * k

        @pl.when(z >= k)
        def _():
            if not finish:
                arrived(low)
            one(z < depth - 1, 0, me + 4, low)
            one(me >= 0, 2, across, low)
            one(me >= 0, 3, beside, low)

        @pl.when(z + k < depth)
        def _():
            if not finish:
                arrived(high)
            one(z > 0, 1, me - 4, high)
            one(me >= 0, 2, across, high)
            one(me >= 0, 3, beside, high)

    def other_line(k, finish):
        slot = k * 4 + (q + 2) % 4
        copy = basis_copy(3, slot, beside)
        if finish:
            copy.wait_send()
        else:
            arrived(slot)
            copy.start()

    def others_in(k):
        arrived(k * 4 + beside % 4)
        arrived(k * 4 + (beside + 2) % 4)

    loads[0].wait()
    own_out(False)
    gath[me] = ba[0]
    loads[1].wait()

    offset = lax.broadcasted_iota(jnp.int32, (blk, blk), 0) - lax.broadcasted_iota(
        jnp.int32, (blk, blk), 1
    )
    inside = jnp.abs(offset) <= BAND
    for b in range(blocks):
        for p in range(2):
            part = jnp.where(inside, di[b, p].astype(F32), 0.0)
            ds[b, p * blk : (p + 1) * blk, 0:blk] = part.astype(BF16)
            other = part if p == 0 else -part
            ds[b, (1 - p) * blk : (2 - p) * blk, blk:two] = other.astype(BF16)

    def near_block(b):
        for j in range(tiles):
            place, held = jnp.int32(0), jnp.int32(0)
            for m in range(near):
                hit = (nt[b, m] == j).astype(jnp.int32)
                place = jnp.maximum(place, m * hit)
                held = jnp.maximum(held, hit)
            keep = held.astype(F32)
            for p in range(2):
                piece = cp[b, place, p].astype(F32) * keep
                nn[p * blk : (p + 1) * blk, j * tile : (j + 1) * tile] = piece.astype(BF16)
        whole = mul(ds[b], nn[...]).astype(BF16)
        for i in range(blocks):
            at = slice(i * blk, (i + 1) * blk)
            w[span(b), col(i) : col(i) + blk] = whole[0:blk, at]
            w[span(b), col(i) + blk : col(i) + two] = whole[blk:two, at]

    loads[2].wait()
    near_block(0)
    for k in range(1, blocks):
        line(k, False)
        near_block(k)

    def line_loop(k, carry):
        line(k, False)
        return carry

    lax.fori_loop(blocks, depth, line_loop, 0)

    def other_loop(k, carry):
        other_line(k, False)
        return carry

    lax.fori_loop(0, depth, other_loop, 0)

    for load in loads[3:]:
        load.wait()
    for t in range(0, ticks, batch):
        wide = slice(t * columns, (t + batch) * columns)
        for b in range(blocks):
            both = mul(ds[b, :, 0:blk], rs[b * blk : (b + 1) * blk, wide])
            for k in range(batch):
                y[t + k, span(b), :] = complex_sum(both[:, k * columns : (k + 1) * columns])

    def others_loop(k, carry):
        others_in(k)
        return carry

    lax.fori_loop(0, depth, others_loop, 0)

    for b in range(blocks):
        real, imag = gath[fb[b, 0], 0], gath[fb[b, 0], 1]
        bd[b, :, 0:two] = jnp.concatenate([real, -imag], axis=1)
        low = jnp.concatenate([imag, real], axis=1)
        both = jnp.concatenate([bd[b, :, 0:two], low], axis=0)
        pair = mul(both, ds[b, :, 0:blk]).astype(BF16)
        bd[b, :, two : two + blk] = pair[0:rank]
        bd[b, :, two + blk : 2 * two] = pair[rank : 2 * rank]

    for t in range(0, ticks, batch):
        wide = slice(t * columns, (t + batch) * columns)
        both = jnp.zeros((2 * rank, batch * columns), F32)
        for b in range(blocks):
            pair = jnp.concatenate(
                [bd[b, :, two : two + blk], bd[b, :, two + blk : 2 * two]], axis=0
            )
            both = both + mul(pair, rs[b * blk : (b + 1) * blk, wide])
        for k in range(batch):
            y[t + k, extra, :] = complex_sum(both[:, k * columns : (k + 1) * columns])

    def chain_copy(t, c):
        at = pl.ds(first(c), sent(c))
        return pltpu.make_async_remote_copy(
            src_ref=sbuf.at[t, at],
            dst_ref=vbuf.at[t, at],
            send_sem=cs.at[t, c],
            recv_sem=cr.at[t, c],
            device_id={"slab": me + 1},
            device_id_type=MESH,
        )

    def out_copy(t, c):
        return pltpu.make_async_copy(
            sbuf.at[t, pl.ds(first(c), blk)], out.at[t, pl.ds(c * blk, blk)], outs.at[t, c]
        )

    def give(t, c, values):
        sbuf[t, first(c) : first(c) + sent(c), :] = values.astype(BF16)

        @pl.when(me < n - 1)
        def _():
            chain_copy(t, c).start()

        out_copy(t, c).start()

    @pl.when(me == 0)
    def _():
        def tick(t, carry):
            for b in range(blocks):
                give(t, b, y[t, first(b) : first(b) + sent(b), :])
            return carry

        lax.fori_loop(0, ticks, tick, 0)

    @pl.when(me > 0)
    def _():
        for b in range(blocks):
            real, imag = gath[fb[b, 1], 0], gath[fb[b, 1], 1]
            far = jnp.concatenate(
                [
                    jnp.concatenate([real, imag], axis=1),
                    jnp.concatenate([imag, -real], axis=1),
                ],
                axis=0,
            )
            spread = lax.dot_general(
                ds[b, 0:blk, :], far, (((1,), (1,)), ((), ())), preferred_element_type=F32
            )
            w[span(b), extra_col] = (spread * scale[0]).astype(BF16)

        for i in range(blocks):
            total = jnp.zeros((2 * rank, blk), F32)
            for b in range(blocks):
                up = bd[b, :, 0:two]
                down = jnp.concatenate([-up[:, blk:two], up[:, 0:blk]], axis=1)
                stack = jnp.concatenate(
                    [w[span(b), col(i) : col(i) + blk], w[span(b), col(i) + blk : col(i) + two]],
                    axis=0,
                )
                total = total + mul(jnp.concatenate([up, down], axis=0), stack)
            w[extra, col(i) : col(i) + blk] = total[0:rank].astype(BF16)
            w[extra, col(i) + blk : col(i) + two] = total[rank : 2 * rank].astype(BF16)
        total = jnp.zeros((rank, 2 * rank), F32)
        for b in range(blocks):
            spread = w[span(b), extra_col]
            swapped = turned(spread.astype(F32)).astype(BF16)
            total = total + mul(bd[b, :, 0:blk], spread) - mul(bd[b, :, blk:two], swapped)
        w[extra, extra_col] = total.astype(BF16)

        def tick(t, carry):
            for c in range(blocks):
                chain_copy(t, c).wait_recv()
                piece = vbuf[t, span(c), :]
                parts = [piece, turned(piece.astype(F32)).astype(BF16)]
                if c == 0:
                    field = vbuf[t, extra, :].astype(F32)
                    parts += [field.astype(BF16), turned(field).astype(BF16)]
                state = jnp.concatenate(parts, axis=0)
                cols = slice(col(c), col(c) + state.shape[0])
                if c < blocks - 1:
                    old = y[t] if c == 0 else acc[...]
                    acc[...] = old - mul(w[:, cols], state)
                    if c == 0:
                        acc[extra, :] = acc[extra, :] + field
                else:
                    for b in range(blocks):
                        at = slice(first(b), first(b) + sent(b))
                        give(t, b, acc[at, :] - mul(w[at, cols], state))
            return carry

        lax.fori_loop(0, ticks, tick, 0)

    def chain_end(t, carry):
        for c in range(blocks):
            out_copy(t, c).wait()

            @pl.when(me < n - 1)
            def _():
                chain_copy(t, c).wait_send()

        return carry

    lax.fori_loop(0, ticks, chain_end, 0)

    own_out(True)

    def line_end(k, carry):
        line(k, True)
        return carry

    lax.fori_loop(1, depth, line_end, 0)

    def other_end(k, carry):
        other_line(k, True)
        return carry

    lax.fori_loop(0, depth, other_end, 0)


def body(right_side, coupling, diag_inverse, basis, near_tiles, far_basis):
    blocks, _, _, blk, _ = coupling.shape
    ticks, rows, columns = right_side.shape
    rank = basis.shape[2]
    n = lax.axis_size("slab")
    earlier = blocks * jnp.maximum(lax.axis_index("slab"), 1)
    scale = (1.0 / jnp.sqrt(earlier.astype(F32))).reshape(1)
    anywhere = pl.BlockSpec(memory_space=pl.ANY)
    smem = pl.BlockSpec(memory_space=pltpu.SMEM)
    return pl.pallas_call(
        functools.partial(kernel, n),
        out_shape=jax.ShapeDtypeStruct(right_side.shape, right_side.dtype),
        in_specs=[anywhere] * 4 + [smem] * 3,
        out_specs=anywhere,
        scratch_shapes=[
            pltpu.VMEM((rows, ticks * columns), BF16),
            pltpu.VMEM(coupling.shape, BF16),
            pltpu.VMEM(diag_inverse.shape, BF16),
            pltpu.VMEM(basis.shape, BF16),
            pltpu.VMEM((n,) + basis.shape[1:], BF16),
            pltpu.VMEM((rows + rank, 2 * (rows + rank)), BF16),
            pltpu.VMEM((blocks, 2 * blk, 2 * blk), BF16),
            pltpu.VMEM((blocks, rank, 4 * blk), BF16),
            pltpu.VMEM((2 * blk, rows), BF16),
            pltpu.VMEM((ticks, rows + rank, columns), F32),
            pltpu.VMEM((rows + rank, columns), F32),
            pltpu.VMEM((ticks, rows + rank, columns), BF16),
            pltpu.VMEM((ticks, rows + rank, columns), BF16),
            pltpu.SemaphoreType.DMA((4, n)),
            pltpu.SemaphoreType.DMA((n,)),
            pltpu.SemaphoreType.DMA((ticks, blocks)),
            pltpu.SemaphoreType.DMA((ticks, blocks)),
            pltpu.SemaphoreType.DMA((3 + ticks,)),
            pltpu.SemaphoreType.DMA((ticks, blocks)),
        ],
        compiler_params=pltpu.CompilerParams(
            collective_id=0, has_side_effects=True, vmem_limit_bytes=60 * 1024 * 1024
        ),
    )(right_side, coupling, diag_inverse, basis, near_tiles, far_basis, scale)


def solution(mesh):
    placed = (
        P("grp", "slab", None),
        P(("grp", "slab"), None, None, None, None),
        P(("grp", "slab"), None, None, None),
        P(("grp", "slab"), None, None, None),
        P("slab", None),
        P("slab", None),
    )
    return jax.shard_map(
        body, mesh=mesh, in_specs=placed, out_specs=P("grp", "slab", None), check_vma=False
    )
```

```python
import functools

import jax
import jax.numpy as jnp
from jax import lax
from jax.experimental import pallas as pl
from jax.experimental.pallas import tpu as pltpu
from jax.sharding import PartitionSpec as P

BAND = 32
MESH = pl.DeviceIdType.MESH
F32 = jnp.float32
BF16 = jnp.bfloat16


def turned(values):
    half = values.shape[-1] // 2
    rolled = pltpu.roll(values, half, 1)
    lane = lax.broadcasted_iota(jnp.int32, values.shape, 1)
    return jnp.where(lane < half, -rolled, rolled)


def complex_sum(stacked):
    rows = stacked.shape[0] // 2
    return stacked[:rows] + turned(stacked[rows:])


def mul(a, b):
    return jnp.dot(a, b, preferred_element_type=F32)


def kernel(
    n, rs_in, cp_in, di_in, ba_in, nt, fb, scale, out,
    rs, cp, di, ba, gath, w, ds, bd, nn, y, acc, vbuf, sbuf, gs, gr, cs, cr, inn, outs,
):
    loads = [
        pltpu.make_async_copy(src, dst, inn.at[k])
        for k, (src, dst) in enumerate(((ba_in, ba), (di_in, di), (cp_in, cp)))
    ] + [
        pltpu.make_async_copy(
            rs_in.at[t], rs.at[:, pl.ds(t * rs_in.shape[2], rs_in.shape[2])], inn.at[3 + t]
        )
        for t in range(rs_in.shape[0])
    ]
    for load in loads:
        load.start()
    blocks, near, _, blk, tile = cp.shape
    ticks, rows, columns = rs_in.shape
    batch = 4 if ticks % 4 == 0 else 1
    rank = ba.shape[2]
    tiles = rows // tile
    two = 2 * blk
    me = lax.axis_index("slab")
    depth = n // 4
    z, q = me // 4, me % 4
    across = z * 4 + (q + 2) % 4
    beside = me + 1 - 2 * (q % 2)

    def first(b):
        return b * blk + (rank if b else 0)

    def span(b):
        return slice(first(b), first(b) + blk)

    def sent(b):
        return blk if b else blk + rank

    def col(b):
        return b * two + (2 * rank if b else 0)

    extra = slice(blk, blk + rank)
    extra_col = slice(two, two + 2 * rank)
    barrier = pltpu.get_barrier_semaphore()

    def greet(there, who):
        @pl.when(there)
        def _():
            pl.semaphore_signal(barrier, inc=1, device_id={"slab": who}, device_id_type=MESH)

    sides = (
        (me > 0, me - 1),
        (me < n - 1, me + 1),
        (z > 0, me - 4),
        (z < depth - 1, me + 4),
        (me >= 0, across),
    )
    for there, who in sides:
        greet(there, who)
    pl.semaphore_wait(barrier, sum(there.astype(jnp.int32) for there, _ in sides))

    def basis_copy(way, slot, who, own=False):
        return pltpu.make_async_remote_copy(
            src_ref=ba.at[0] if own else gath.at[slot],
            dst_ref=gath.at[slot],
            send_sem=gs.at[way, slot],
            recv_sem=gr.at[slot],
            device_id={"slab": who},
            device_id_type=MESH,
        )

    def arrived(slot):
        basis_copy(0, slot, beside).wait_recv()

    def own_out(finish):
        def one(there, way, who):
            @pl.when(there)
            def _():
                copy = basis_copy(way, me, who, own=True)
                copy.wait_send() if finish else copy.start()

        one(z < depth - 1, 0, me + 4)
        one(z > 0, 1, me - 4)
        one(me >= 0, 2, across)
        one(me >= 0, 3, beside)

    def line(k, finish):
        def one(there, way, who, slot):
            @pl.when(there)
            def _():
                copy = basis_copy(way, slot, who)
                copy.wait_send() if finish else copy.start()

        low, high = me - 4 * k, me + 4 * k

        @pl.when(z >= k)
        def _():
            if not finish:
                arrived(low)
            one(z < depth - 1, 0, me + 4, low)
            one(me >= 0, 2, across, low)
            one(me >= 0, 3, beside, low)

        @pl.when(z + k < depth)
        def _():
            if not finish:
                arrived(high)
            one(z > 0, 1, me - 4, high)
            one(me >= 0, 2, across, high)
            one(me >= 0, 3, beside, high)

    def other_line(k, finish):
        slot = k * 4 + (q + 2) % 4
        copy = basis_copy(3, slot, beside)
        if finish:
            copy.wait_send()
        else:
            arrived(slot)
            copy.start()

    def others_in(k):
        arrived(k * 4 + beside % 4)
        arrived(k * 4 + (beside + 2) % 4)

    loads[0].wait()
    own_out(False)
    gath[me] = ba[0]
    loads[1].wait()

    offset = lax.broadcasted_iota(jnp.int32, (blk, blk), 0) - lax.broadcasted_iota(
        jnp.int32, (blk, blk), 1
    )
    inside = jnp.abs(offset) <= BAND
    for b in range(blocks):
        for p in range(2):
            part = jnp.where(inside, di[b, p].astype(F32), 0.0)
            ds[b, p * blk : (p + 1) * blk, 0:blk] = part.astype(BF16)
            other = part if p == 0 else -part
            ds[b, (1 - p) * blk : (2 - p) * blk, blk:two] = other.astype(BF16)

    def near_block(b):
        for j in range(tiles):
            place, held = jnp.int32(0), jnp.int32(0)
            for m in range(near):
                hit = (nt[b, m] == j).astype(jnp.int32)
                place = jnp.maximum(place, m * hit)
                held = jnp.maximum(held, hit)
            keep = held.astype(F32)
            for p in range(2):
                piece = cp[b, place, p].astype(F32) * keep
                nn[p * blk : (p + 1) * blk, j * tile : (j + 1) * tile] = piece.astype(BF16)
        whole = mul(ds[b], nn[...]).astype(BF16)
        for i in range(blocks):
            at = slice(i * blk, (i + 1) * blk)
            w[span(b), col(i) : col(i) + blk] = whole[0:blk, at]
            w[span(b), col(i) + blk : col(i) + two] = whole[blk:two, at]

    loads[2].wait()
    near_block(0)
    for k in range(1, blocks):
        line(k, False)
        near_block(k)

    def line_loop(k, carry):
        line(k, False)
        return carry

    lax.fori_loop(blocks, depth, line_loop, 0)

    def other_loop(k, carry):
        other_line(k, False)
        return carry

    lax.fori_loop(0, depth, other_loop, 0)

    for load in loads[3:]:
        load.wait()
    for t in range(0, ticks, batch):
        wide = slice(t * columns, (t + batch) * columns)
        for b in range(blocks):
            both = mul(ds[b, :, 0:blk], rs[b * blk : (b + 1) * blk, wide])
            for k in range(batch):
                y[t + k, span(b), :] = complex_sum(both[:, k * columns : (k + 1) * columns])

    def others_loop(k, carry):
        others_in(k)
        return carry

    lax.fori_loop(0, depth, others_loop, 0)

    for b in range(blocks):
        real, imag = gath[fb[b, 0], 0], gath[fb[b, 0], 1]
        bd[b, :, 0:two] = jnp.concatenate([real, -imag], axis=1)
        low = jnp.concatenate([imag, real], axis=1)
        both = jnp.concatenate([bd[b, :, 0:two], low], axis=0)
        pair = mul(both, ds[b, :, 0:blk]).astype(BF16)
        bd[b, :, two : two + blk] = pair[0:rank]
        bd[b, :, two + blk : 2 * two] = pair[rank : 2 * rank]

    for t in range(0, ticks, batch):
        wide = slice(t * columns, (t + batch) * columns)
        both = jnp.zeros((2 * rank, batch * columns), F32)
        for b in range(blocks):
            pair = jnp.concatenate(
                [bd[b, :, two : two + blk], bd[b, :, two + blk : 2 * two]], axis=0
            )
            both = both + mul(pair, rs[b * blk : (b + 1) * blk, wide])
        for k in range(batch):
            y[t + k, extra, :] = complex_sum(both[:, k * columns : (k + 1) * columns])

    def chain_copy(t, c):
        at = pl.ds(first(c), sent(c))
        return pltpu.make_async_remote_copy(
            src_ref=sbuf.at[t, at],
            dst_ref=vbuf.at[t, at],
            send_sem=cs.at[t, c],
            recv_sem=cr.at[t, c],
            device_id={"slab": me + 1},
            device_id_type=MESH,
        )

    def out_copy(t, c):
        return pltpu.make_async_copy(
            sbuf.at[t, pl.ds(first(c), blk)], out.at[t, pl.ds(c * blk, blk)], outs.at[t, c]
        )

    def give(t, c, values):
        sbuf[t, first(c) : first(c) + sent(c), :] = values.astype(BF16)

        @pl.when(me < n - 1)
        def _():
            chain_copy(t, c).start()

        out_copy(t, c).start()

    @pl.when(me == 0)
    def _():
        def tick(t, carry):
            for b in range(blocks):
                give(t, b, y[t, first(b) : first(b) + sent(b), :])
            return carry

        lax.fori_loop(0, ticks, tick, 0)

    @pl.when(me > 0)
    def _():
        for b in range(blocks):
            real, imag = gath[fb[b, 1], 0], gath[fb[b, 1], 1]
            far = jnp.concatenate(
                [
                    jnp.concatenate([real, imag], axis=1),
                    jnp.concatenate([imag, -real], axis=1),
                ],
                axis=0,
            )
            spread = lax.dot_general(
                ds[b, 0:blk, :], far, (((1,), (1,)), ((), ())), preferred_element_type=F32
            )
            w[span(b), extra_col] = (spread * scale[0]).astype(BF16)

        for i in range(blocks):
            total = jnp.zeros((2 * rank, blk), F32)
            for b in range(blocks):
                up = bd[b, :, 0:two]
                down = jnp.concatenate([-up[:, blk:two], up[:, 0:blk]], axis=1)
                stack = jnp.concatenate(
                    [w[span(b), col(i) : col(i) + blk], w[span(b), col(i) + blk : col(i) + two]],
                    axis=0,
                )
                total = total + mul(jnp.concatenate([up, down], axis=0), stack)
            w[extra, col(i) : col(i) + blk] = total[0:rank].astype(BF16)
            w[extra, col(i) + blk : col(i) + two] = total[rank : 2 * rank].astype(BF16)
        total = jnp.zeros((rank, 2 * rank), F32)
        for b in range(blocks):
            spread = w[span(b), extra_col]
            swapped = turned(spread.astype(F32)).astype(BF16)
            total = total + mul(bd[b, :, 0:blk], spread) - mul(bd[b, :, blk:two], swapped)
        w[extra, extra_col] = total.astype(BF16)

        def piece(t, c):
            own = vbuf[t, span(c), :]
            parts = [own, turned(own.astype(F32)).astype(BF16)]
            if c == 0:
                field = vbuf[t, extra, :]
                parts += [field, turned(field.astype(F32)).astype(BF16)]
            return parts

        last = col(blocks - 1)

        def tick(t, carry):
            parts = []
            for c in range(blocks - 1):
                chain_copy(t, c).wait_recv()
                parts += piece(t, c)
            acc[...] = y[t] - mul(w[:, 0:last], jnp.concatenate(parts, axis=0))
            acc[extra, :] = acc[extra, :] + vbuf[t, extra, :].astype(F32)
            chain_copy(t, blocks - 1).wait_recv()
            tail = jnp.concatenate(piece(t, blocks - 1), axis=0)
            done = acc[...] - mul(w[:, last : last + two], tail)
            for b in range(blocks):
                give(t, b, done[first(b) : first(b) + sent(b), :])
            return carry

        lax.fori_loop(0, ticks, tick, 0)

    def chain_end(t, carry):
        for c in range(blocks):
            out_copy(t, c).wait()

            @pl.when(me < n - 1)
            def _():
                chain_copy(t, c).wait_send()

        return carry

    lax.fori_loop(0, ticks, chain_end, 0)

    own_out(True)

    def line_end(k, carry):
        line(k, True)
        return carry

    lax.fori_loop(1, depth, line_end, 0)

    def other_end(k, carry):
        other_line(k, True)
        return carry

    lax.fori_loop(0, depth, other_end, 0)


def body(right_side, coupling, diag_inverse, basis, near_tiles, far_basis):
    blocks, _, _, blk, _ = coupling.shape
    ticks, rows, columns = right_side.shape
    rank = basis.shape[2]
    n = lax.axis_size("slab")
    earlier = blocks * jnp.maximum(lax.axis_index("slab"), 1)
    scale = (1.0 / jnp.sqrt(earlier.astype(F32))).reshape(1)
    anywhere = pl.BlockSpec(memory_space=pl.ANY)
    smem = pl.BlockSpec(memory_space=pltpu.SMEM)
    return pl.pallas_call(
        functools.partial(kernel, n),
        out_shape=jax.ShapeDtypeStruct(right_side.shape, right_side.dtype),
        in_specs=[anywhere] * 4 + [smem] * 3,
        out_specs=anywhere,
        scratch_shapes=[
            pltpu.VMEM((rows, ticks * columns), BF16),
            pltpu.VMEM(coupling.shape, BF16),
            pltpu.VMEM(diag_inverse.shape, BF16),
            pltpu.VMEM(basis.shape, BF16),
            pltpu.VMEM((n,) + basis.shape[1:], BF16),
            pltpu.VMEM((rows + rank, 2 * (rows + rank)), BF16),
            pltpu.VMEM((blocks, 2 * blk, 2 * blk), BF16),
            pltpu.VMEM((blocks, rank, 4 * blk), BF16),
            pltpu.VMEM((2 * blk, rows), BF16),
            pltpu.VMEM((ticks, rows + rank, columns), F32),
            pltpu.VMEM((rows + rank, columns), F32),
            pltpu.VMEM((ticks, rows + rank, columns), BF16),
            pltpu.VMEM((ticks, rows + rank, columns), BF16),
            pltpu.SemaphoreType.DMA((4, n)),
            pltpu.SemaphoreType.DMA((n,)),
            pltpu.SemaphoreType.DMA((ticks, blocks)),
            pltpu.SemaphoreType.DMA((ticks, blocks)),
            pltpu.SemaphoreType.DMA((3 + ticks,)),
            pltpu.SemaphoreType.DMA((ticks, blocks)),
        ],
        compiler_params=pltpu.CompilerParams(
            collective_id=0, has_side_effects=True, vmem_limit_bytes=60 * 1024 * 1024
        ),
    )(right_side, coupling, diag_inverse, basis, near_tiles, far_basis, scale)


def solution(mesh):
    placed = (
        P("grp", "slab", None),
        P(("grp", "slab"), None, None, None, None),
        P(("grp", "slab"), None, None, None),
        P(("grp", "slab"), None, None, None),
        P("slab", None),
        P("slab", None),
    )
    return jax.shard_map(
        body, mesh=mesh, in_specs=placed, out_specs=P("grp", "slab", None), check_vma=False
    )
```
